32 devices in a mesh: facet: 4 (over z), col: 8 (over y, x, core).
Axes of the slice: x: 2, y: 2, z: 4, core: 2. Of those that a mesh axis runs over, the one named last changes fastest.
Arguments:
- sky_re: bfloat16 [4, 4096, 4096], P('facet', None, 'col'), may hold values from -6 to 6
- sky_im: bfloat16 [4, 4096, 4096], P('facet', None, 'col'), may hold values from -6 to 6
- col_offsets: int32 [2], replicated, may hold values from 0 to 65280
- sub_offsets: int32 [4], replicated, may hold values from 0 to 65280
- kernel: float32 [16, 8], replicated, may hold values from 0.05 to 1
- vis_count: int32 [4, 32], P('facet', 'col'), may hold values from 0 to 128, as said below
- cell_index: int32 [2, 4, 32, 128], P(None, 'facet', 'col'), may hold values from 0 to 248
- frac_index: int32 [2, 4, 32, 128], P(None, 'facet', 'col'), may hold values from 0 to 15
Outputs:
- vis_re: float32 [4, 32, 128], P('facet', 'col')
- vis_im: float32 [4, 32, 128], P('facet', 'col')
The draws below stay inside these ranges and needn't reach their ends.
Inputs may be any that keep to these rules, and one draw needn't show every extreme that they name: Within each subgrid the blocks with visibilities come first and block 0 holds 128; in some subgrid all 32 blocks hold visibilities; a block's visibilities fill its first vis_count slots.
All inputs are finite; a program needn't handle non-finite values.
Results may differ from the reference program's by a relative error of at most 0.0037.
Values may be sent and summed in bfloat16 or wider, within the bound.
A program may use at most 64 MiB of HBM per device.

```python
import math
import jax
import jax.numpy as jnp
from jax import lax

N_IMG = 65536
M = 4096
S = 256
KS = 8
OS = 16
SCOL = 2
VB = 128
NSUB = 4
BLK_SUB = 32
N_FACET = 4


def draw_vis_count(key, part):
    key_full, key_live, key_counts = jax.random.split(jax.random.fold_in(key, 11), 3)
    full_index = jax.random.randint(key_full, (), 0, NSUB)
    raw_draws = jax.random.randint(key_live, (NSUB,), 1, BLK_SUB + 1)
    live_blocks = jnp.maximum(1, raw_draws * raw_draws // BLK_SUB)
    live_blocks = jnp.where(jnp.arange(NSUB) == full_index, BLK_SUB, live_blocks)
    counts = jax.random.randint(key_counts, (NSUB, BLK_SUB), 1, VB + 1)
    block_ids = jnp.arange(BLK_SUB)[None, :]
    counts = jnp.where(block_ids == 0, VB, counts)
    return jnp.where(block_ids < live_blocks[:, None], counts, 0).astype(jnp.int32)


def place_ends(drawn, own_key, smallest, top_value):
    shape = drawn.shape
    index_at = [jax.random.randint(jax.random.fold_in(own_key, axis), (), 0, shape[axis]) for axis in range(len(shape))]
    drawn = drawn.at[tuple(index_at)].set(smallest)
    longest = shape.index(max(shape))
    index_at[longest] = (index_at[longest] + 1) % shape[longest]
    return drawn.at[tuple(index_at)].set(top_value)


def level_of(rng, extent, shards, smallest, high):
    def one(axis_at, shards_of):
        draws = jax.random.uniform(jax.random.fold_in(jax.random.fold_in(rng, 6), axis_at), (shards_of,), jnp.float32, smallest / len(shards), high / len(shards))
        return jnp.repeat(jnp.exp(draws), extent[axis_at] // shards_of).reshape((-1,) + (1,) * (len(extent) - axis_at - 1))

    level = one(*shards[0])
    for cut in shards[1:]:
        level = level * one(*cut)
    return level


def centred(stream_key, shape, scale, bound, cuts=(), kind=jnp.bfloat16):
    array = jax.random.normal(stream_key, shape, jnp.float32) * scale
    if len(cuts) > 0:
        array = level_of(stream_key, shape, cuts, -0.22, 0.18) * array
    return jnp.clip(array, min=-bound, max=bound).astype(kind)


def setup_inputs(seed: int = 0) -> dict:
    arg_keys = jax.random.split(jax.random.key(seed), 9)
    sky_re = centred(arg_keys[0], (N_FACET, M, M), 1.0, 6.0, ((0, 4), (2, 8)))
    sky_im = centred(arg_keys[1], (N_FACET, M, M), 1.0, 6.0, ((0, 4), (2, 8)))
    col_offsets = jax.random.randint(arg_keys[2], (SCOL,), 0, N_IMG - S + 1).astype(jnp.int32)
    sub_offsets = place_ends(jax.random.randint(arg_keys[3], (NSUB,), 0, N_IMG - S + 1), jax.random.fold_in(arg_keys[3], 1), 0, N_IMG - S).astype(jnp.int32)
    kernel = jnp.clip(jnp.exp(jax.random.uniform(arg_keys[4], (OS, KS), jnp.float32, math.log(0.05), math.log(1.0))), 0.05, 1.0)
    vis_count = draw_vis_count(jax.random.fold_in(arg_keys[8], 71), 0)
    cell_index = place_ends(jax.random.randint(arg_keys[6], (2, NSUB, BLK_SUB, VB), 0, S - KS + 1), jax.random.fold_in(arg_keys[6], 1), 0, S - KS).astype(jnp.int32)
    frac_index = place_ends(jax.random.randint(arg_keys[7], (2, NSUB, BLK_SUB, VB), 0, OS), jax.random.fold_in(arg_keys[7], 1), 0, OS - 1).astype(jnp.int32)
    return {"sky_re": sky_re, "sky_im": sky_im, "col_offsets": col_offsets, "sub_offsets": sub_offsets, "kernel": kernel, "vis_count": vis_count, "cell_index": cell_index, "frac_index": frac_index}


def modular_product(left_ints, right_ints):
    upper_part = right_ints // 256
    lower_part = right_ints % 256
    product = left_ints[:, None] * upper_part[None, :] % N_IMG
    product = product * 256 % N_IMG
    return (product + left_ints[:, None] * lower_part[None, :]) % N_IMG

def cos_sin(left_ints, right_ints, factor):
    angles = modular_product(left_ints, right_ints).astype(jnp.float32) * (2.0 * math.pi / N_IMG)
    return (jnp.cos(angles) * factor, jnp.sin(angles) * factor)

def first_axis(facet_image, table, local_cols):
    product = jnp.dot(table, facet_image, preferred_element_type=jnp.float32)
    real_part = product[:S, :local_cols] + product[S:, local_cols:]
    imag_part = product[:S, local_cols:] - product[S:, :local_cols]
    return jnp.stack([real_part, imag_part]).astype(jnp.bfloat16)

def second_axis(band_rows, starts, anchor, second_table):
    mod_cos, mod_sin = cos_sin(starts, anchor, 1.0)
    shifted_re = band_rows[0][None] * mod_cos[:, None] + band_rows[1][None] * mod_sin[:, None]
    shifted_im = band_rows[1][None] * mod_cos[:, None] - band_rows[0][None] * mod_sin[:, None]
    stacked = jnp.concatenate([shifted_re, shifted_im], axis=0).astype(jnp.bfloat16)
    per_column = starts.shape[0]
    row_count = band_rows.shape[1]
    product = jnp.dot(stacked.reshape(2 * per_column * row_count, -1), second_table, preferred_element_type=jnp.float32)
    product = product.reshape(2, per_column, row_count, 2 * S)
    term_re = product[0, :, :, :S] + product[1, :, :, S:]
    term_im = product[1, :, :, :S] - product[0, :, :, S:]
    return jnp.concatenate([term_re, term_im], axis=2)

def lookup(frac_ints, kernel):
    table_rows = jnp.arange(kernel.shape[0], dtype=jnp.int32)
    matches = frac_ints[..., None] == table_rows
    return lax.optimization_barrier(jnp.sum(jnp.where(matches[..., None], kernel, 0.0), axis=-2))

def reference(sky_re, sky_im, col_offsets, sub_offsets, kernel, vis_count, cell_index, frac_index):
    spatial = jnp.arange(M, dtype=jnp.int32)
    spectral = jnp.arange(S, dtype=jnp.int32)
    per_column = NSUB // SCOL
    first_tables = []
    for column in range(SCOL):
        cos_part, sin_part = cos_sin(col_offsets[column] + spectral, spatial, 1.0 / math.sqrt(M))
        first_tables.append(jnp.concatenate([cos_part, sin_part], axis=0).astype(jnp.bfloat16))

    def facet_step(running, inputs):
        real_part, imag_part, facet_index = inputs
        facet_image = jnp.concatenate([real_part, imag_part], axis=1)
        anchor = facet_index * M + spatial
        cos_tab, sin_tab = cos_sin(anchor, spectral, 1.0 / math.sqrt(M * N_FACET))
        second_table = jnp.concatenate([cos_tab, sin_tab], axis=1).astype(jnp.bfloat16)
        column_terms = []
        for column in range(SCOL):
            band_rows = first_axis(facet_image, first_tables[column], M)
            starts = sub_offsets[column * per_column:(column + 1) * per_column]
            column_terms.append(second_axis(band_rows, starts, anchor, second_table))
        return (running + jnp.concatenate(column_terms, axis=0), None)
    initial = jnp.zeros((NSUB, S, 2 * S), jnp.float32)
    subgrids, _ = lax.scan(facet_step, initial, (sky_re, sky_im, jnp.arange(N_FACET, dtype=jnp.int32)))
    subgrids = subgrids.astype(jnp.bfloat16)
    offsets = jnp.arange(KS, dtype=jnp.int32)
    slot_ids = jnp.arange(VB, dtype=jnp.int32)

    def one_subgrid(inputs):
        subgrid, cell_rows, frac_rows, counts = inputs

        def one_block(block_inputs):
            cell_block, frac_block, slot_count = block_inputs
            row_taps = lookup(frac_block[0], kernel).astype(jnp.bfloat16)
            row_taps = lax.optimization_barrier(row_taps).astype(jnp.float32)
            col_taps = lookup(frac_block[1], kernel)
            gathered = jnp.take(subgrid, cell_block[0][:, None] + offsets, axis=0).astype(jnp.float32)
            row_sum = jnp.einsum('va,vac->vc', row_taps, gathered, precision=lax.Precision.HIGHEST)
            col_ids = cell_block[1][:, None] + offsets
            picked_re = jnp.take_along_axis(row_sum[:, :S], col_ids, axis=1)
            picked_im = jnp.take_along_axis(row_sum[:, S:], col_ids, axis=1)
            in_block = slot_ids < slot_count
            vis_real = jnp.where(in_block, lax.optimization_barrier(jnp.sum(picked_re * col_taps, axis=1)), 0.0)
            vis_imag = jnp.where(in_block, lax.optimization_barrier(jnp.sum(picked_im * col_taps, axis=1)), 0.0)
            return (vis_real, vis_imag)
        return lax.map(one_block, (jnp.moveaxis(cell_rows, 1, 0), jnp.moveaxis(frac_rows, 1, 0), counts))
    vis_real, vis_imag = lax.map(one_subgrid, (subgrids, jnp.moveaxis(cell_index, 1, 0), jnp.moveaxis(frac_index, 1, 0), vis_count))
    return (vis_real, vis_imag)
```

```python
import math

import jax
import jax.numpy as jnp
from jax import lax
from jax.sharding import PartitionSpec as P

N_IMG = 65536
S = 256
SCOL = 2


def modular_product(left_ints, right_ints):
    upper_part = right_ints // 256
    lower_part = right_ints % 256
    product = left_ints[:, None] * upper_part[None, :] % N_IMG
    product = product * 256 % N_IMG
    return (product + left_ints[:, None] * lower_part[None, :]) % N_IMG


def cos_sin(left_ints, right_ints, factor):
    angles = modular_product(left_ints, right_ints).astype(jnp.float32) * (2.0 * math.pi / N_IMG)
    return (jnp.cos(angles) * factor, jnp.sin(angles) * factor)


def split_table(left_ints, right_ints, factor):
    parts = 64
    coarse_cos, coarse_sin = cos_sin(left_ints[::parts], right_ints, factor)
    fine_cos, fine_sin = cos_sin(left_ints[:parts] - left_ints[0], right_ints, 1.0)
    cos_tab = coarse_cos[:, None] * fine_cos[None] - coarse_sin[:, None] * fine_sin[None]
    sin_tab = coarse_sin[:, None] * fine_cos[None] + coarse_cos[:, None] * fine_sin[None]
    return (cos_tab.reshape(left_ints.shape[0], -1), sin_tab.reshape(left_ints.shape[0], -1))


def first_axis(facet_image, table, local_cols):
    product = lax.dot_general(
        table, facet_image, (((0,), (0,)), ((), ())), preferred_element_type=jnp.float32
    )
    real_part = product[:S, :local_cols] + product[S:, local_cols:]
    imag_part = product[:S, local_cols:] - product[S:, :local_cols]
    return jnp.stack([real_part, imag_part]).astype(jnp.bfloat16)


def second_axis(band_rows, starts, anchor, second_table):
    mod_cos, mod_sin = cos_sin(starts, anchor, 1.0)
    shifted_re = band_rows[0][None] * mod_cos[:, None] + band_rows[1][None] * mod_sin[:, None]
    shifted_im = band_rows[1][None] * mod_cos[:, None] - band_rows[0][None] * mod_sin[:, None]
    stacked = jnp.concatenate([shifted_re, shifted_im], axis=0).astype(jnp.bfloat16)
    per_column = starts.shape[0]
    row_count = band_rows.shape[1]
    product = jnp.dot(
        stacked.reshape(2 * per_column * row_count, -1),
        second_table,
        preferred_element_type=jnp.float32,
    )
    product = product.reshape(2, per_column, row_count, 2 * S)
    term_re = product[0, :, :, :S] + product[1, :, :, S:]
    term_im = product[1, :, :, :S] - product[0, :, :, S:]
    return jnp.concatenate([term_re, term_im], axis=2)


def lookup(frac_ints, kernel):
    table_rows = jnp.arange(kernel.shape[0], dtype=jnp.int32)
    matches = frac_ints[..., None] == table_rows
    return jnp.sum(jnp.where(matches[..., None], kernel, 0.0), axis=-2)


def spread(cell_ints, tap_values):
    columns = jnp.arange(S, dtype=jnp.int32)
    summed = jnp.zeros(cell_ints.shape + (S,), jnp.float32)
    for offset in range(tap_values.shape[-1]):
        summed = summed + jnp.where(
            columns == cell_ints[..., None] + offset, tap_values[..., offset : offset + 1], 0.0
        )
    return summed


def visibilities(row_sum, col_weights, in_block):
    vis_real = jnp.where(in_block, jnp.sum(row_sum[..., :S] * col_weights, axis=-1), 0.0)
    vis_imag = jnp.where(in_block, jnp.sum(row_sum[..., S:] * col_weights, axis=-1), 0.0)
    return (vis_real, vis_imag)


def facet_table(facet_anchor, spectral, pixels, facets):
    cos_tab, sin_tab = split_table(facet_anchor, spectral, 1.0 / math.sqrt(pixels * facets))
    return jnp.concatenate([cos_tab, sin_tab], axis=1).astype(jnp.bfloat16)


def local(sky_re, sky_im, col_offsets, sub_offsets, kernel, vis_count, cell_index, frac_index):
    pixels = sky_re.shape[1]
    local_cols = sky_re.shape[2]
    facets = lax.axis_size("facet")
    per_column = sub_offsets.shape[0] // SCOL
    owned = vis_count.shape[0]
    facet_image = jnp.concatenate([sky_re[0], sky_im[0]], axis=1)
    spatial = jnp.arange(pixels, dtype=jnp.int32)
    spectral = jnp.arange(S, dtype=jnp.int32)

    def column_table(column):
        cos_part, sin_part = split_table(
            spatial, col_offsets[column] + spectral, 1.0 / math.sqrt(pixels)
        )
        return jnp.concatenate([cos_part, sin_part], axis=1).astype(jnp.bfloat16)

    def column_starts(column):
        return sub_offsets[column * per_column : (column + 1) * per_column]

    pieces = jnp.stack(
        [first_axis(facet_image, column_table(column), local_cols) for column in range(SCOL)]
    )
    received = lax.all_to_all(pieces, "col", split_axis=2, concat_axis=3, tiled=True)
    column_bands = [received[column] for column in range(SCOL)]
    anchor = lax.axis_index("facet") * pixels + spatial
    second_table = facet_table(anchor, spectral, pixels, facets)
    column_terms = [
        second_axis(column_bands[column], column_starts(column), anchor, second_table)
        for column in range(SCOL)
    ]
    partial_value = jnp.concatenate(column_terms, axis=0)
    grid_rows = lax.psum_scatter(partial_value, "facet", scatter_dimension=0, tiled=True).astype(
        jnp.bfloat16
    )
    blocks = vis_count.shape[1]
    block_slots = cell_index.shape[-1]
    slot_ids = jnp.arange(block_slots, dtype=jnp.int32)
    row_weights = spread(cell_index[0], lookup(frac_index[0], kernel)).astype(jnp.bfloat16)
    row_weights = row_weights.reshape(owned, blocks * block_slots, S)
    col_weights = spread(cell_index[1], lookup(frac_index[1], kernel)).reshape(
        owned, blocks * block_slots, S
    )
    row_sum = jnp.einsum(
        "svr,src->svc",
        row_weights,
        lax.all_gather(grid_rows, "col", axis=1, tiled=True),
        preferred_element_type=jnp.float32,
    )
    in_block = (slot_ids < vis_count[..., None]).reshape(owned, blocks * block_slots)
    flat_re, flat_im = visibilities(row_sum, col_weights, in_block)
    vis_real = flat_re.reshape(owned, blocks, block_slots)
    vis_imag = flat_im.reshape(owned, blocks, block_slots)
    return (vis_real, vis_imag)


def solution(mesh):
    placed = (
        P("facet", None, "col"),
        P("facet", None, "col"),
        P(),
        P(),
        P(),
        P("facet", "col"),
        P(None, "facet", "col", None),
        P(None, "facet", "col", None),
    )
    return jax.shard_map(
        local,
        mesh=mesh,
        in_specs=placed,
        out_specs=(P("facet", "col", None), P("facet", "col", None)),
        check_vma=False,
    )
```

```python
import functools
import math

import jax
import jax.numpy as jnp
from jax import lax
from jax.experimental import pallas as pl
from jax.experimental.pallas import tpu as pltpu
from jax.sharding import PartitionSpec as P

N_IMG = 65536
MASK = N_IMG - 1
S = 256
SCOL = 2
LANES = 128
F32 = jnp.float32
BF16 = jnp.bfloat16


def unit(points):
    angles = points.astype(F32) * (2.0 * math.pi / N_IMG)
    return jnp.cos(angles), jnp.sin(angles)


def times(left, right):
    return (
        left[0] * right[0] - left[1] * right[1],
        left[0] * right[1] + left[1] * right[0],
    )


def iota(shape, dim):
    return lax.broadcasted_iota(jnp.int32, shape, dim)


def exclusive(left, right, count):
    total, bit = 0, 1
    while bit < count:
        total = total + ((left // bit) % 2 + (right // bit) % 2) % 2 * bit
        bit *= 2
    return total


def body(
    dims,
    coff_ref,
    soff_ref,
    kern_ref,
    count_ref,
    cell_ref,
    frac_ref,
    re_hbm,
    im_hbm,
    vre_ref,
    vim_ref,
    sky,
    table,
    prod,
    base,
    shift_tab,
    second,
    stacked,
    prod2,
    sendbuf,
    recv,
    zbuf,
    zrecv,
    grid,
    row_w,
    col_w,
    taps,
    sky_sem,
    send_sem,
    recv_sem,
    zsend_sem,
    zrecv_sem,
    gsend_sem,
    grecv_sem,
):
    n_f, n_c, pixels, cols, subs, owned, blocks, slots, groups, ksize, over = dims
    rows = S // groups
    rp = S // n_c
    dpg = n_c // groups
    per = subs // SCOL
    f = lax.axis_index("facet")
    c = lax.axis_index("col")

    loads = []
    for index, src in enumerate((re_hbm, im_hbm)):
        copy = pltpu.make_async_copy(
            src.at[0], sky.at[index], sky_sem.at[index]
        )
        copy.start()
        loads.append(copy)

    barrier = pltpu.get_barrier_semaphore()
    for step in range(1, n_c):
        pl.semaphore_signal(barrier, inc=1, device_id={"col": lax.rem(c + step, n_c)})
    for step in range(1, n_f):
        pl.semaphore_signal(barrier, inc=1, device_id={"facet": lax.rem(f + step, n_f)})

    jrow = iota((rows, LANES), 0)
    lane = iota((rows, LANES), 1)
    base[0], base[1] = unit(jrow * lane)
    base[2], base[3] = unit((jrow * LANES) & MASK)

    first_y = f * pixels + c * cols
    ycol = first_y + iota((subs, cols), 1)
    soff = soff_ref[...]
    points = ((soff * (ycol // 256)) & MASK) * 256 + soff * (ycol % 256)
    shift_tab[0], shift_tab[1] = unit(points & MASK)

    strip = 32
    kline = iota((strip, S), 1)
    mline = first_y + iota((strip, S), 0)
    points = ((mline // 256 * kline) & MASK) * 256 + (mline % 256) * kline
    now = unit(points & MASK)
    scale2 = 1.0 / math.sqrt(pixels * n_f)
    now = (now[0] * scale2, now[1] * scale2)
    stride = unit((strip * iota((8, S), 1)) & MASK)
    stride = (stride[0][0:1], stride[1][0:1])
    for part in range(cols // strip):
        here = slice(part * strip, (part + 1) * strip)
        second[here, :S] = now[0].astype(BF16)
        second[here, S:] = now[1].astype(BF16)
        now = times(now, stride)

    own_group = c // dpg
    scale1 = 1.0 / math.sqrt(pixels)

    def send(dest):
        return pltpu.make_async_remote_copy(
            src_ref=sendbuf.at[dest],
            dst_ref=recv.at[c],
            send_sem=send_sem.at[dest],
            recv_sem=recv_sem.at[c],
            device_id={"col": dest},
        )

    def fill_table(g):
        for q in range(SCOL):
            start = coff_ref[q] + g * rows
            ll = iota((8, LANES), 1)
            along = unit((start * ll) & MASK)
            along = (along[0][0:1] * scale1, along[1][0:1] * scale1)
            jump = unit((start * LANES + 0 * ll) & MASK)
            jump = (jump[0][0:1], jump[1][0:1])
            now = times((base[0], base[1]), along)
            jump = times((base[2], base[3]), jump)
            top = q * 2 * rows
            for part in range(pixels // LANES):
                lanes = slice(part * LANES, (part + 1) * LANES)
                table[top : top + rows, lanes] = now[0].astype(BF16)
                table[top + rows : top + 2 * rows, lanes] = now[1].astype(BF16)
                now = times(now, jump)

    def transform(g):
        for index in range(2):
            prod[:, index * cols : (index + 1) * cols] = jnp.dot(
                table[...], sky[index], preferred_element_type=F32
            )
        for q in range(SCOL):
            cos_rows = slice(q * 2 * rows, q * 2 * rows + rows)
            sin_rows = slice(q * 2 * rows + rows, (q + 1) * 2 * rows)
            band_re = prod[cos_rows, :cols] + prod[sin_rows, cols:]
            band_im = prod[cos_rows, cols:] - prod[sin_rows, :cols]
            band_re = band_re.astype(BF16).astype(F32)
            band_im = band_im.astype(BF16).astype(F32)
            for s in range(q * per, (q + 1) * per):
                sc = shift_tab[0, s : s + 1]
                sd = shift_tab[1, s : s + 1]
                at = s * 2 * rows
                stacked[at : at + rows] = (band_re * sc + band_im * sd).astype(BF16)
                stacked[at + rows : at + 2 * rows] = (band_im * sc - band_re * sd).astype(BF16)
        prod2[...] = jnp.dot(stacked[...], second[...], preferred_element_type=F32)
        for s in range(subs):
            for t in range(dpg):
                upper = slice(s * 2 * rows + t * rp, s * 2 * rows + (t + 1) * rp)
                lower = slice(upper.start + rows, upper.stop + rows)
                dest = g * dpg + t
                sendbuf[dest, s, :, :S] = (prod2[upper, :S] + prod2[lower, S:]).astype(BF16)
                sendbuf[dest, s, :, S:] = (prod2[lower, :S] - prod2[upper, S:]).astype(BF16)

    def group_at(step):
        return exclusive(own_group, groups - 1 - step, groups)

    fill_table(group_at(0))
    for copy in loads:
        copy.wait()
    transform(group_at(0))
    pl.semaphore_wait(barrier, n_c - 1 + n_f - 1)

    def one_group(step, carry):
        fill_table(group_at(step))
        for t in range(dpg):
            send(group_at(step - 1) * dpg + t).start()
        transform(group_at(step))
        return carry

    lax.fori_loop(1, groups, one_group, 0)

    total = owned * blocks
    frac = frac_ref[...]
    for tap in range(ksize):
        value = jnp.zeros(frac.shape, F32)
        for row in range(over):
            value = jnp.where(frac == row, kern_ref[row, tap], value)
        taps[tap] = value

    for t in range(dpg - 1):
        send(own_group * dpg + lax.rem(lax.rem(c, dpg) + 1 + t, dpg)).start()

    for b in range(total):
        lanes = slice(b * slots, (b + 1) * slots)
        away_row = iota((S, slots), 0) - cell_ref[b : b + 1]
        away_col = iota((S, slots), 0) - cell_ref[total + b : total + b + 1]
        row_val = jnp.zeros((S, slots), F32)
        col_val = jnp.zeros((S, slots), F32)
        for tap in range(ksize):
            row_val = jnp.where(away_row == tap, taps[tap, b : b + 1], row_val)
            col_val = jnp.where(away_col == tap, taps[tap, total + b : total + b + 1], col_val)
        row_w[:, lanes] = row_val.astype(BF16)
        col_w[:, lanes] = col_val

    for step in range(1, n_c):
        src = lax.rem(c + step, n_c)
        pltpu.make_async_remote_copy(
            src_ref=recv.at[src],
            dst_ref=recv.at[src],
            send_sem=send_sem.at[src],
            recv_sem=recv_sem.at[src],
            device_id={"col": src},
        ).wait_recv()
    for s in range(subs):
        acc = sendbuf[c, s].astype(F32)
        for step in range(1, n_c):
            acc = acc + recv[lax.rem(c + step, n_c), s].astype(F32)
        zbuf[s // owned, s % owned] = acc.astype(BF16)

    def zcopy(dest):
        return pltpu.make_async_remote_copy(
            src_ref=zbuf.at[dest],
            dst_ref=zrecv.at[f],
            send_sem=zsend_sem.at[dest],
            recv_sem=zrecv_sem.at[f],
            device_id={"facet": dest},
        )

    for step in range(1, n_f):
        zcopy(lax.rem(f + step, n_f)).start()
    for step in range(1, n_c):
        send(lax.rem(c + step, n_c)).wait_send()
    for step in range(1, n_f):
        src = lax.rem(f + step, n_f)
        pltpu.make_async_remote_copy(
            src_ref=zrecv.at[src],
            dst_ref=zrecv.at[src],
            send_sem=zsend_sem.at[src],
            recv_sem=zrecv_sem.at[src],
            device_id={"facet": src},
        ).wait_recv()
    acc = zbuf[f].astype(F32)
    for step in range(1, n_f):
        acc = acc + zrecv[lax.rem(f + step, n_f)].astype(F32)
    grid[c] = acc.astype(BF16)

    def gcopy(dest):
        return pltpu.make_async_remote_copy(
            src_ref=grid.at[c],
            dst_ref=grid.at[c],
            send_sem=gsend_sem.at[dest],
            recv_sem=grecv_sem.at[c],
            device_id={"col": dest},
        )

    for step in range(1, n_c):
        gcopy(lax.rem(c + step, n_c)).start()
    for step in range(1, n_f):
        zcopy(lax.rem(f + step, n_f)).wait_send()
    for step in range(1, n_c):
        src = lax.rem(c + step, n_c)
        pltpu.make_async_remote_copy(
            src_ref=grid.at[src],
            dst_ref=grid.at[src],
            send_sem=gsend_sem.at[src],
            recv_sem=grecv_sem.at[src],
            device_id={"col": src},
        ).wait_recv()
    for step in range(1, n_c):
        gcopy(lax.rem(c + step, n_c)).wait_send()

    for o in range(owned):
        cells = grid[:, o]
        if rp % 16 == 0:
            cells = cells.reshape(S, 2 * S)
        else:
            cells = cells.astype(F32).reshape(S, 2 * S).astype(BF16)
        for b in range(o * blocks, (o + 1) * blocks):
            lanes = slice(b * slots, (b + 1) * slots)
            summed = lax.dot_general(
                cells,
                row_w[:, lanes],
                (((0,), (0,)), ((), ())),
                preferred_element_type=F32,
            )
            weights = col_w[:, lanes]
            live = iota((1, slots), 1) < count_ref[b]
            vis_real = jnp.sum(summed[:S] * weights, axis=0, keepdims=True)
            vis_imag = jnp.sum(summed[S:] * weights, axis=0, keepdims=True)
            vre_ref[b : b + 1] = jnp.where(live, vis_real, 0.0)
            vim_ref[b : b + 1] = jnp.where(live, vis_imag, 0.0)


def local(sky_re, sky_im, col_offsets, sub_offsets, kernel, vis_count, cell_index, frac_index):
    n_f = lax.axis_size("facet")
    n_c = lax.axis_size("col")
    pixels, cols = sky_re.shape[1:]
    subs = sub_offsets.shape[0]
    owned, blocks = vis_count.shape
    slots = cell_index.shape[-1]
    over, ksize = kernel.shape
    groups = 4
    rows = S // groups
    rp = S // n_c
    total = owned * blocks
    dims = (n_f, n_c, pixels, cols, subs, owned, blocks, slots, groups, ksize, over)
    smem = pl.BlockSpec(memory_space=pltpu.SMEM)
    vmem = pl.BlockSpec(memory_space=pltpu.VMEM)
    anywhere = pl.BlockSpec(memory_space=pl.ANY)
    dma = pltpu.SemaphoreType.DMA
    out = jax.ShapeDtypeStruct((total, slots), F32)
    vis_real, vis_imag = pl.pallas_call(
        functools.partial(body, dims),
        out_shape=(out, out),
        in_specs=[smem, vmem, smem, smem, vmem, vmem, anywhere, anywhere],
        out_specs=(vmem, vmem),
        scratch_shapes=[
            pltpu.VMEM((2, pixels, cols), BF16),
            pltpu.VMEM((2 * SCOL * rows, pixels), BF16),
            pltpu.VMEM((2 * SCOL * rows, 2 * cols), F32),
            pltpu.VMEM((4, rows, LANES), F32),
            pltpu.VMEM((2, subs, cols), F32),
            pltpu.VMEM((cols, 2 * S), BF16),
            pltpu.VMEM((2 * subs * rows, cols), BF16),
            pltpu.VMEM((2 * subs * rows, 2 * S), F32),
            pltpu.VMEM((n_c, subs, rp, 2 * S), BF16),
            pltpu.VMEM((n_c, subs, rp, 2 * S), BF16),
            pltpu.VMEM((n_f, owned, rp, 2 * S), BF16),
            pltpu.VMEM((n_f, owned, rp, 2 * S), BF16),
            pltpu.VMEM((n_c, owned, rp, 2 * S), BF16),
            pltpu.VMEM((S, total * slots), BF16),
            pltpu.VMEM((S, total * slots), F32),
            pltpu.VMEM((ksize, 2 * total, slots), F32),
            dma((2,)),
            dma((n_c,)),
            dma((n_c,)),
            dma((n_f,)),
            dma((n_f,)),
            dma((n_c,)),
            dma((n_c,)),
        ],
        compiler_params=pltpu.CompilerParams(
            collective_id=0, has_side_effects=True, vmem_limit_bytes=56 << 20
        ),
    )(
        col_offsets,
        sub_offsets.reshape(subs, 1),
        kernel,
        vis_count.reshape(total),
        cell_index.reshape(2 * total, slots),
        frac_index.reshape(2 * total, slots),
        sky_re,
        sky_im,
    )
    shape = (owned, blocks, slots)
    return (vis_real.reshape(shape), vis_imag.reshape(shape))


def solution(mesh):
    placed = (
        P("facet", None, "col"),
        P("facet", None, "col"),
        P(),
        P(),
        P(),
        P("facet", "col"),
        P(None, "facet", "col", None),
        P(None, "facet", "col", None),
    )
    return jax.shard_map(
        local,
        mesh=mesh,
        in_specs=placed,
        out_specs=(P("facet", "col", None), P("facet", "col", None)),
        check_vma=False,
    )
```

```python
import functools
import math

import jax
import jax.numpy as jnp
from jax import lax
from jax.experimental import pallas as pl
from jax.experimental.pallas import tpu as pltpu
from jax.sharding import PartitionSpec as P

N_IMG = 65536
MASK = N_IMG - 1
S = 256
SCOL = 2
LANES = 128
F32 = jnp.float32
BF16 = jnp.bfloat16


def unit(points):
    angles = points.astype(F32) * (2.0 * math.pi / N_IMG)
    return jnp.cos(angles), jnp.sin(angles)


def times(left, right):
    return (
        left[0] * right[0] - left[1] * right[1],
        left[0] * right[1] + left[1] * right[0],
    )


def iota(shape, dim):
    return lax.broadcasted_iota(jnp.int32, shape, dim)


def exclusive(left, right, count):
    total, bit = 0, 1
    while bit < count:
        total = total + ((left // bit) % 2 + (right // bit) % 2) % 2 * bit
        bit *= 2
    return total


def body(
    dims,
    coff_ref,
    soff_ref,
    kern_ref,
    count_ref,
    cell_ref,
    frac_ref,
    re_hbm,
    im_hbm,
    vis_ref,
    sky,
    table_a,
    table_b,
    prod,
    base,
    shift_tab,
    second,
    stacked,
    prod2,
    sendbuf,
    recv,
    zbuf,
    zrecv,
    grid,
    row_w,
    col_w,
    taps,
    sky_sem,
    send_sem,
    recv_sem,
    zsend_sem,
    zrecv_sem,
    gsend_sem,
    grecv_sem,
):
    n_f, n_c, pixels, cols, subs, owned, blocks, slots, groups, ksize, over = dims
    rows = S // groups
    rp = S // n_c
    dpg = n_c // groups
    per = subs // SCOL
    f = lax.axis_index("facet")
    c = lax.axis_index("col")

    loads = []
    for index, src in enumerate((re_hbm, im_hbm)):
        copy = pltpu.make_async_copy(
            src.at[0], sky.at[index], sky_sem.at[index]
        )
        copy.start()
        loads.append(copy)

    barrier = pltpu.get_barrier_semaphore()
    for step in range(1, n_c):
        pl.semaphore_signal(barrier, inc=1, device_id={"col": lax.rem(c + step, n_c)})
    for step in range(1, n_f):
        pl.semaphore_signal(barrier, inc=1, device_id={"facet": lax.rem(f + step, n_f)})

    jrow = iota((rows, LANES), 0)
    lane = iota((rows, LANES), 1)
    base[0], base[1] = unit(jrow * lane)
    base[2], base[3] = unit((jrow * LANES) & MASK)

    first_y = f * pixels + c * cols
    ycol = first_y + iota((subs, cols), 1)
    srow = iota((subs, cols), 0)
    soff = jnp.zeros((subs, cols), jnp.int32)
    for s in range(subs):
        soff = jnp.where(srow == s, soff_ref[s], soff)
    points = ((soff * (ycol // 256)) & MASK) * 256 + soff * (ycol % 256)
    shift_tab[0], shift_tab[1] = unit(points & MASK)

    strip = 32
    kline = iota((strip, S), 1)
    mline = first_y + iota((strip, S), 0)
    points = ((mline // 256 * kline) & MASK) * 256 + (mline % 256) * kline
    now = unit(points & MASK)
    scale2 = 1.0 / math.sqrt(pixels * n_f)
    now = (now[0] * scale2, now[1] * scale2)
    stride = unit((strip * iota((8, S), 1)) & MASK)
    stride = (stride[0][0:1], stride[1][0:1])
    for part in range(cols // strip):
        here = slice(part * strip, (part + 1) * strip)
        second[here, :S] = now[0].astype(BF16)
        second[here, S:] = now[1].astype(BF16)
        now = times(now, stride)

    own_group = c // dpg
    scale1 = 1.0 / math.sqrt(pixels)

    def send(dest):
        return pltpu.make_async_remote_copy(
            src_ref=sendbuf.at[dest],
            dst_ref=recv.at[c],
            send_sem=send_sem.at[dest],
            recv_sem=recv_sem.at[c],
            device_id={"col": dest},
        )

    def fill_table(table, g, columns):
        for q in columns:
            start = coff_ref[q] + g * rows
            ll = iota((8, LANES), 1)
            along = unit((start * ll) & MASK)
            along = (along[0][0:1] * scale1, along[1][0:1] * scale1)
            jump = unit((start * LANES + 0 * ll) & MASK)
            jump = (jump[0][0:1], jump[1][0:1])
            now = times((base[0], base[1]), along)
            jump = times((base[2], base[3]), jump)
            top = q * 2 * rows
            for part in range(pixels // LANES):
                lanes = slice(part * LANES, (part + 1) * LANES)
                table[top : top + rows, lanes] = now[0].astype(BF16)
                table[top + rows : top + 2 * rows, lanes] = now[1].astype(BF16)
                now = times(now, jump)

    def transform(table, g, prepare):
        for index in range(2):
            prepare(index)
            prod[:, index * cols : (index + 1) * cols] = jnp.dot(
                table[...], sky[index], preferred_element_type=F32
            )
        for q in range(SCOL):
            cos_rows = slice(q * 2 * rows, q * 2 * rows + rows)
            sin_rows = slice(q * 2 * rows + rows, (q + 1) * 2 * rows)
            band_re = prod[cos_rows, :cols] + prod[sin_rows, cols:]
            band_im = prod[cos_rows, cols:] - prod[sin_rows, :cols]
            band_re = band_re.astype(BF16).astype(F32)
            band_im = band_im.astype(BF16).astype(F32)
            for s in range(q * per, (q + 1) * per):
                sc = shift_tab[0, s : s + 1]
                sd = shift_tab[1, s : s + 1]
                at = s * 2 * rows
                stacked[at : at + rows] = (band_re * sc + band_im * sd).astype(BF16)
                stacked[at + rows : at + 2 * rows] = (band_im * sc - band_re * sd).astype(BF16)
        prod2[...] = jnp.dot(stacked[...], second[...], preferred_element_type=F32)
        for s in range(subs):
            for t in range(dpg):
                upper = slice(s * 2 * rows + t * rp, s * 2 * rows + (t + 1) * rp)
                lower = slice(upper.start + rows, upper.stop + rows)
                dest = g * dpg + t
                sendbuf[dest, s, :, :S] = (prod2[upper, :S] + prod2[lower, S:]).astype(BF16)
                sendbuf[dest, s, :, S:] = (prod2[lower, :S] - prod2[upper, S:]).astype(BF16)

    def group_at(step):
        return exclusive(own_group, groups - 1 - step, groups)

    tables = (table_a, table_b)
    fill_table(tables[0], group_at(0), range(SCOL))
    for step in range(groups):

        def prepare(index, step=step):
            if step == 0:
                loads[index].wait()
            if step + 1 < groups:
                fill_table(
                    tables[(step + 1) % 2], group_at(step + 1), range(index, SCOL, 2)
                )
            if index == 0 and step > 0:
                for t in range(dpg):
                    send(group_at(step - 1) * dpg + t).start()

        transform(tables[step % 2], group_at(step), prepare)
        if step == 0:
            pl.semaphore_wait(barrier, n_c - 1 + n_f - 1)

    total = owned * blocks
    frac = frac_ref[...]
    for tap in range(ksize):
        value = jnp.zeros(frac.shape, F32)
        for row in range(over):
            value = jnp.where(frac == row, kern_ref[tap, row], value)
        taps[tap] = value

    for t in range(dpg - 1):
        send(own_group * dpg + lax.rem(lax.rem(c, dpg) + 1 + t, dpg)).start()

    for b in range(total):
        lanes = slice(b * slots, (b + 1) * slots)
        away_row = iota((S, slots), 0) - cell_ref[b : b + 1]
        away_col = iota((S, slots), 0) - cell_ref[total + b : total + b + 1]
        row_val = jnp.zeros((S, slots), F32)
        col_val = jnp.zeros((S, slots), F32)
        for tap in range(ksize):
            row_val = jnp.where(away_row == tap, taps[tap, b : b + 1], row_val)
            col_val = jnp.where(away_col == tap, taps[tap, total + b : total + b + 1], col_val)
        row_w[:, lanes] = row_val.astype(BF16)
        col_w[:, lanes] = col_val

    for step in range(1, n_c):
        src = lax.rem(c + step, n_c)
        pltpu.make_async_remote_copy(
            src_ref=recv.at[src],
            dst_ref=recv.at[src],
            send_sem=send_sem.at[src],
            recv_sem=recv_sem.at[src],
            device_id={"col": src},
        ).wait_recv()
    for s in range(subs):
        acc = sendbuf[c, s].astype(F32)
        for step in range(1, n_c):
            acc = acc + recv[lax.rem(c + step, n_c), s].astype(F32)
        zbuf[s // owned, s % owned] = acc.astype(BF16)

    def zcopy(dest):
        return pltpu.make_async_remote_copy(
            src_ref=zbuf.at[dest],
            dst_ref=zrecv.at[f],
            send_sem=zsend_sem.at[dest],
            recv_sem=zrecv_sem.at[f],
            device_id={"facet": dest},
        )

    for step in range(1, n_f):
        zcopy(lax.rem(f + step, n_f)).start()
    for step in range(1, n_c):
        send(lax.rem(c + step, n_c)).wait_send()
    for step in range(1, n_f):
        src = lax.rem(f + step, n_f)
        pltpu.make_async_remote_copy(
            src_ref=zrecv.at[src],
            dst_ref=zrecv.at[src],
            send_sem=zsend_sem.at[src],
            recv_sem=zrecv_sem.at[src],
            device_id={"facet": src},
        ).wait_recv()
    acc = zbuf[f].astype(F32)
    for step in range(1, n_f):
        acc = acc + zrecv[lax.rem(f + step, n_f)].astype(F32)
    grid[c] = acc.astype(BF16)

    def gcopy(dest):
        return pltpu.make_async_remote_copy(
            src_ref=grid.at[c],
            dst_ref=grid.at[c],
            send_sem=gsend_sem.at[dest],
            recv_sem=grecv_sem.at[c],
            device_id={"col": dest},
        )

    for step in range(1, n_c):
        gcopy(lax.rem(c + step, n_c)).start()
    for step in range(1, n_f):
        zcopy(lax.rem(f + step, n_f)).wait_send()
    for step in range(1, n_c):
        src = lax.rem(c + step, n_c)
        pltpu.make_async_remote_copy(
            src_ref=grid.at[src],
            dst_ref=grid.at[src],
            send_sem=gsend_sem.at[src],
            recv_sem=grecv_sem.at[src],
            device_id={"col": src},
        ).wait_recv()
    for step in range(1, n_c):
        gcopy(lax.rem(c + step, n_c)).wait_send()

    for o in range(owned):
        cells = grid[:, o]
        if rp % 16 == 0:
            cells = cells.reshape(S, 2 * S)
        else:
            cells = cells.astype(F32).reshape(S, 2 * S).astype(BF16)
        for b in range(o * blocks, (o + 1) * blocks):
            lanes = slice(b * slots, (b + 1) * slots)
            summed = lax.dot_general(
                cells,
                row_w[:, lanes],
                (((0,), (0,)), ((), ())),
                preferred_element_type=F32,
            )
            weights = col_w[:, lanes]
            live = iota((1, slots), 1) < count_ref[b]
            vis_real = jnp.sum(summed[:S] * weights, axis=0, keepdims=True)
            vis_imag = jnp.sum(summed[S:] * weights, axis=0, keepdims=True)
            vis_ref[b : b + 1] = jnp.where(live, vis_real, 0.0)
            vis_ref[total + b : total + b + 1] = jnp.where(live, vis_imag, 0.0)


def local(sky_re, sky_im, col_offsets, sub_offsets, kernel, vis_count, cell_index, frac_index):
    n_f = lax.axis_size("facet")
    n_c = lax.axis_size("col")
    pixels, cols = sky_re.shape[1:]
    subs = sub_offsets.shape[0]
    owned, blocks = vis_count.shape
    slots = cell_index.shape[-1]
    over, ksize = kernel.shape
    groups = 4
    rows = S // groups
    rp = S // n_c
    total = owned * blocks
    dims = (n_f, n_c, pixels, cols, subs, owned, blocks, slots, groups, ksize, over)
    smem = pl.BlockSpec(memory_space=pltpu.SMEM)
    vmem = pl.BlockSpec(memory_space=pltpu.VMEM)
    anywhere = pl.BlockSpec(memory_space=pl.ANY)
    dma = pltpu.SemaphoreType.DMA
    out = jax.ShapeDtypeStruct((2 * total, slots), F32)
    vis = pl.pallas_call(
        functools.partial(body, dims),
        out_shape=out,
        in_specs=[smem, smem, smem, smem, vmem, vmem, anywhere, anywhere],
        out_specs=vmem,
        scratch_shapes=[
            pltpu.VMEM((2, pixels, cols), BF16),
            pltpu.VMEM((2 * SCOL * rows, pixels), BF16),
            pltpu.VMEM((2 * SCOL * rows, pixels), BF16),
            pltpu.VMEM((2 * SCOL * rows, 2 * cols), F32),
            pltpu.VMEM((4, rows, LANES), F32),
            pltpu.VMEM((2, subs, cols), F32),
            pltpu.VMEM((cols, 2 * S), BF16),
            pltpu.VMEM((2 * subs * rows, cols), BF16),
            pltpu.VMEM((2 * subs * rows, 2 * S), F32),
            pltpu.VMEM((n_c, subs, rp, 2 * S), BF16),
            pltpu.VMEM((n_c, subs, rp, 2 * S), BF16),
            pltpu.VMEM((n_f, owned, rp, 2 * S), BF16),
            pltpu.VMEM((n_f, owned, rp, 2 * S), BF16),
            pltpu.VMEM((n_c, owned, rp, 2 * S), BF16),
            pltpu.VMEM((S, total * slots), BF16),
            pltpu.VMEM((S, total * slots), F32),
            pltpu.VMEM((ksize, 2 * total, slots), F32),
            dma((2,)),
            dma((n_c,)),
            dma((n_c,)),
            dma((n_f,)),
            dma((n_f,)),
            dma((n_c,)),
            dma((n_c,)),
        ],
        compiler_params=pltpu.CompilerParams(
            collective_id=0, has_side_effects=True, vmem_limit_bytes=56 << 20
        ),
    )(
        col_offsets,
        sub_offsets,
        kernel.T,
        vis_count.reshape(total),
        cell_index.reshape(2 * total, slots),
        frac_index.reshape(2 * total, slots),
        sky_re,
        sky_im,
    )
    vis = vis.reshape(2, owned, blocks, slots)
    return (vis[0], vis[1])


def solution(mesh):
    placed = (
        P("facet", None, "col"),
        P("facet", None, "col"),
        P(),
        P(),
        P(),
        P("facet", "col"),
        P(None, "facet", "col", None),
        P(None, "facet", "col", None),
    )
    return jax.shard_map(
        local,
        mesh=mesh,
        in_specs=placed,
        out_specs=(P("facet", "col", None), P("facet", "col", None)),
        check_vma=False,
    )
```
